32 devices in a mesh: dp: 8 (over z, x), tensor: 4 (over y, core).
Axes of the slice: x: 2, y: 2, z: 4, core: 2. Of those that a mesh axis runs over, the one named last changes fastest.
Arguments:
- hidden_in: bfloat16 [8192, 768], P('dp'), may hold values from -6 to 6
- w_qkv: bfloat16 [3, 768, 768], P(None, None, 'tensor'), may hold values from -0.21875 to 0.21875
- w_out: bfloat16 [768, 768], P('tensor'), may hold values from -0.625 to 0.625
- w_ff1: bfloat16 [768, 768], P(None, 'tensor'), may hold values from -0.21875 to 0.21875
- w_ff2: bfloat16 [768, 768], P('tensor'), may hold values from -0.21875 to 0.21875
- ln1_gain: float32 [768], replicated, may hold values from 0.5 to 1.5
- ln1_bias: float32 [768], replicated, may hold values from -3 to 3
- ln2_gain: float32 [768], replicated, may hold values from 0.5 to 1.5
- ln2_bias: float32 [768], replicated, may hold values from -3 to 3
- spd_table: float32 [32, 32], P(None, 'tensor'), may hold values from -3 to 3
- edge_table: float32 [32, 32], P(None, 'tensor'), may hold values from -3 to 3
- kernel_w1: bfloat16 [128, 128], replicated, may hold values from -0.5 to 0.5
- kernel_w2: bfloat16 [128, 32], P(None, 'tensor'), may hold values from -0.5 to 0.5
- centers: float32 [128], replicated, may hold values from 0 to 8
- widths: float32 [128], replicated, may hold values from 0.3 to 3
- atom_count: int32 [128], P('dp'), may hold values from 16 to 64, as said below
- mol_mode: int32 [128], P('dp'), may hold values from 0 to 2
- spd_bucket: int32 [128, 64, 64], P('dp'), may hold values from 0 to 31
- edge_type: int32 [128, 64, 64], P('dp'), may hold values from 0 to 31
- dist_bucket: int32 [128, 64, 64], P('dp'), may hold values from 0 to 127
- cotangent: bfloat16 [8192, 768], P('dp'), may hold values from -6 to 6
Outputs:
- layer_out: bfloat16 [8192, 768], P('dp')
- grad_in: bfloat16 [8192, 768], P('dp')
- grad_qkv: float32 [3, 768, 768], P(None, None, 'tensor')
- grad_out: float32 [768, 768], P('tensor')
- grad_ff1: float32 [768, 768], P(None, 'tensor')
- grad_ff2: float32 [768, 768], P('tensor')
- grad_ln1_gain: float32 [768], replicated
- grad_ln1_bias: float32 [768], replicated
- grad_ln2_gain: float32 [768], replicated
- grad_ln2_bias: float32 [768], replicated
- grad_spd: float32 [32, 32], P(None, 'tensor')
- grad_edge: float32 [32, 32], P(None, 'tensor')
- grad_kernel_w1: float32 [128, 128], replicated
- grad_kernel_w2: float32 [128, 32], P(None, 'tensor')
- grad_centers: float32 [128], replicated
- grad_widths: float32 [128], replicated
The draws below stay inside these ranges and needn't reach their ends.
Inputs may be any that keep to these rules, and one draw needn't show every extreme that they name: `atom_count`: every molecule has at least 16 real atoms, and some molecule has exactly 64.
All inputs are finite; a program needn't handle non-finite values.
Results may differ from the reference program's by a relative error of at most 0.02.
Values may be sent and summed in bfloat16 or wider, within the bound.
No kernel may reach another device: no remote copies, remote signals or barrier semaphores. Data moves between devices by JAX's collectives and lax.ppermute only.
A program may use at most 128 MiB of HBM per device.

```python
import math
from functools import partial
import jax
import jax.numpy as jnp
from jax import lax

D = 768
HEADS = 32
HD = 24
FF = 768
KERNELS = 128
SPD = 32
EDGE = 32
DIST = 128
ATOMS = 64
MOLS = 128
TOKENS = 8192


def draw_atom_count(key, part):
    first, second = jax.random.split(jax.random.fold_in(key, 11))
    counts = jax.random.randint(first, (MOLS,), ATOMS // 4, ATOMS + 1)
    chosen = jax.random.randint(second, (), 0, MOLS)
    return jnp.where(jnp.arange(MOLS) == chosen, ATOMS, counts).astype(jnp.int32)


def place_ends(values, rng, least, high):
    spot = [jax.random.randint(jax.random.fold_in(rng, axis), (), 0, length) for axis, length in enumerate(values.shape)]
    widest = values.shape.index(max(values.shape))
    next_to = spot[:widest] + [(spot[widest] + 1) % values.shape[widest]] + spot[widest + 1:]
    return values.at[tuple(spot)].set(least).at[tuple(next_to)].set(high)


def steps_of(key, extent, pieces, least, high):
    level, own = 1.0, jax.random.fold_in(key, 6)
    for axis_at, blocks in pieces:
        draws = jnp.exp(jax.random.uniform(jax.random.fold_in(own, axis_at), (blocks,), jnp.float32, least / len(pieces), high / len(pieces)))
        level = level * jnp.repeat(draws, extent[axis_at] // blocks).reshape([-1 if axis == axis_at else 1 for axis in range(len(extent))])
    return level


def gaussian(rng, dims, width, reach, pieces=(), kind=jnp.bfloat16):
    entries = jax.random.normal(rng, dims, jnp.float32) * width
    if len(pieces) > 0:
        entries = steps_of(rng, dims, pieces, -0.22, 0.18) * entries
    return jnp.clip(entries, min=-reach, max=reach).astype(kind)


def setup_inputs(seed: int = 0) -> dict:
    streams_of = jax.random.split(jax.random.key(seed), 22)
    return {
        "hidden_in": gaussian(streams_of[0], (TOKENS, D), 1.0, 6.0, ((0, 8),)),
        "w_qkv": gaussian(streams_of[1], (3, D, D), D ** -0.5, 0.21875, ((2, 4),)),
        "w_out": gaussian(streams_of[2], (D, D), (D // 8) ** -0.5, 0.625, ((0, 4),)),
        "w_ff1": gaussian(streams_of[3], (D, FF), D ** -0.5, 0.21875, ((1, 4),)),
        "w_ff2": gaussian(streams_of[4], (FF, D), FF ** -0.5, 0.21875, ((0, 4),)),
        "ln1_gain": jnp.clip(1.0 + 0.1 * jax.random.normal(streams_of[5], (D,), jnp.float32), 0.5, 1.5),
        "ln1_bias": gaussian(streams_of[6], (D,), 0.5, 3.0, (), jnp.float32),
        "ln2_gain": jnp.clip(1.0 + 0.1 * jax.random.normal(streams_of[7], (D,), jnp.float32), 0.5, 1.5),
        "ln2_bias": gaussian(streams_of[8], (D,), 0.5, 3.0, (), jnp.float32),
        "spd_table": gaussian(streams_of[9], (SPD, HEADS), 0.5, 3.0, ((1, 4),), jnp.float32),
        "edge_table": gaussian(streams_of[10], (EDGE, HEADS), 0.5, 3.0, ((1, 4),), jnp.float32),
        "kernel_w1": gaussian(streams_of[11], (KERNELS, KERNELS), KERNELS ** -0.5, 0.5),
        "kernel_w2": gaussian(streams_of[12], (KERNELS, HEADS), KERNELS ** -0.5, 0.5, ((1, 4),)),
        "centers": jnp.clip(jax.random.uniform(streams_of[13], (KERNELS,), jnp.float32, 0.0, 8.0), 0.0, 8.0),
        "widths": jnp.clip(jnp.exp(jax.random.uniform(streams_of[14], (KERNELS,), jnp.float32, math.log(0.3), math.log(3.0))), 0.3, 3.0),
        "atom_count": draw_atom_count(jax.random.fold_in(streams_of[21], 71), 0),
        "mol_mode": place_ends(jax.random.randint(streams_of[16], (MOLS,), 0, 3), jax.random.fold_in(streams_of[16], 1), 0, 2).astype(jnp.int32),
        "spd_bucket": place_ends(jax.random.randint(streams_of[17], (MOLS, ATOMS, ATOMS), 0, SPD), jax.random.fold_in(streams_of[17], 1), 0, SPD - 1).astype(jnp.int32),
        "edge_type": place_ends(jax.random.randint(streams_of[18], (MOLS, ATOMS, ATOMS), 0, EDGE), jax.random.fold_in(streams_of[18], 1), 0, EDGE - 1).astype(jnp.int32),
        "dist_bucket": place_ends(jax.random.randint(streams_of[19], (MOLS, ATOMS, ATOMS), 0, DIST), jax.random.fold_in(streams_of[19], 1), 0, DIST - 1).astype(jnp.int32),
        "cotangent": gaussian(streams_of[20], (TOKENS, D), 1.0, 6.0, ((0, 8),)),
    }


eps = 1e-05
neg_fill = -1000000000.0
highest = lax.Precision.HIGHEST

@jax.custom_vjp
def low(v):
    return lax.optimization_barrier(v.astype(jnp.bfloat16)).astype(jnp.float32)

@jax.custom_vjp
def low_back(v):
    return v

def low_keep(v):
    return (low(v), None)

def low_pass(kept, grad):
    return (grad,)

def back_keep(v):
    return (v, None)

def back_low(kept, grad):
    return (low(grad),)
low.defvjp(low_keep, low_pass)
low_back.defvjp(back_keep, back_low)

def norm_rows(values, gain, shift):
    center = values - lax.optimization_barrier(jnp.mean(values, axis=-1, keepdims=True))
    spread = lax.optimization_barrier(jnp.mean(center * center, axis=-1, keepdims=True))
    return center * lax.rsqrt(spread + eps) * gain + shift

def gelu_exact(values):
    return jax.nn.gelu(values, approximate=False)

def kernels(dist, centers, widths):
    place = dist.astype(jnp.float32)[..., None] * (8.0 / DIST)
    offset = (place - centers) / widths
    return jnp.exp(-0.5 * offset * offset) / widths

def matmul(left, right):
    return jnp.dot(left, right, precision=highest)

def attend_group(tables, items):
    spd_table, edge_table, kernel_w1, kernel_w2, centers, widths = tables
    query, keyset, values, count, mode, spd_ids, edge_ids, dist = items
    atoms = query.shape[1]
    two_flag = (mode != 1).astype(jnp.float32)[:, None, None, None]
    three_flag = (mode != 0).astype(jnp.float32)[:, None, None, None]
    flat = matmul(jax.nn.one_hot(spd_ids, SPD, dtype=jnp.float32), spd_table)
    flat = flat + matmul(jax.nn.one_hot(edge_ids, EDGE, dtype=jnp.float32), edge_table)
    basis = low(kernels(dist, centers, widths))
    hidden = low(gelu_exact(low_back(matmul(basis, kernel_w1))))
    geo = matmul(hidden, kernel_w2)
    bias = two_flag * flat + three_flag * geo
    scores = jnp.einsum('gihe,gjhe->ghij', query, keyset, precision=highest)
    scores = low_back(scores + jnp.transpose(bias, (0, 3, 1, 2)))
    keep = (jnp.arange(atoms)[None, :] < count[:, None])[:, None, None, :]
    scores = jnp.where(keep, scores, neg_fill)
    row_max = lax.optimization_barrier(jnp.max(scores, axis=-1, keepdims=True))
    expos = jnp.exp(scores - row_max)
    probs = low(expos / lax.optimization_barrier(jnp.sum(expos, axis=-1, keepdims=True)))
    return jnp.einsum('ghij,gjhe->gihe', probs, values, precision=highest)

def reference(hidden_in, w_qkv, w_out, w_ff1, w_ff2, ln1_gain, ln1_bias, ln2_gain, ln2_bias, spd_table, edge_table, kernel_w1, kernel_w2, centers, widths, atom_count, mol_mode, spd_bucket, edge_type, dist_bucket, cotangent):
    group = math.gcd(MOLS, 64)
    count_groups = MOLS // group

    def split_mols(array):
        return array.reshape((count_groups, group) + array.shape[1:])

    def split_heads(array):
        return array.reshape(count_groups, group, ATOMS, HEADS, HD)
    int_items = (split_mols(atom_count), split_mols(mol_mode), split_mols(spd_bucket), split_mols(edge_type), split_mols(dist_bucket))
    scale = 1.0 / math.sqrt(HD)

    def forward(source, wqkv, wout, wff1, wff2, gain_one, bias_one, gain_two, bias_two, spd_tab, edge_tab, kernel_one, kernel_two, center_v, width_v):
        normed_one = low(norm_rows(source, gain_one, bias_one))
        query = low_back(low(matmul(normed_one, wqkv[0]) * scale))
        keyset = low_back(low(matmul(normed_one, wqkv[1])))
        values = low_back(low(matmul(normed_one, wqkv[2])))
        tables = (spd_tab, edge_tab, kernel_one, kernel_two, center_v, width_v)
        mixed = lax.map(jax.checkpoint(partial(attend_group, tables)), (split_heads(query), split_heads(keyset), split_heads(values)) + int_items)
        mixed = low_back(low(mixed.reshape(TOKENS, D)))
        middle = source + low_back(matmul(mixed, wout))
        normed_two = low(norm_rows(middle, gain_two, bias_two))
        inner = low_back(matmul(normed_two, wff1))
        active = low(gelu_exact(inner))
        return middle + low_back(matmul(active, wff2))
    floats = (hidden_in.astype(jnp.float32), w_qkv.astype(jnp.float32), w_out.astype(jnp.float32), w_ff1.astype(jnp.float32), w_ff2.astype(jnp.float32), ln1_gain, ln1_bias, ln2_gain, ln2_bias, spd_table, edge_table, kernel_w1.astype(jnp.float32), kernel_w2.astype(jnp.float32), centers, widths)
    result, pull = jax.vjp(forward, *floats)
    grads = pull(cotangent.astype(jnp.float32))
    return (result.astype(jnp.bfloat16), grads[0].astype(jnp.bfloat16), grads[1], grads[2], grads[3], grads[4], grads[5], grads[6], grads[7], grads[8], grads[9], grads[10], grads[11], grads[12], grads[13], grads[14])
```

```python
import math

import jax
import jax.numpy as jnp
from jax import lax
from jax.experimental import pallas as pl
from jax.experimental.pallas import tpu as pltpu
from jax.sharding import PartitionSpec as P

EPS = 1e-05
NEG = -1000000000.0
F32 = jnp.float32
BF16 = jnp.bfloat16
NN = (((1,), (0,)), ((), ()))
NT = (((1,), (1,)), ((), ()))
TN = (((0,), (0,)), ((), ()))
CHUNKS = 2
SPD = 32
DIST = 128


def dot(left, right, dims):
    return lax.dot_general(left, right, dims, preferred_element_type=F32)


def cdf(values):
    return 0.5 * (1.0 + lax.erf(values * math.sqrt(0.5)))


def gelu_slope(values, phi):
    return phi + values * jnp.exp(-0.5 * values * values) * (1.0 / math.sqrt(2.0 * math.pi))


def normed(values):
    center = values - jnp.mean(values, axis=-1, keepdims=True)
    rstd = lax.rsqrt(jnp.mean(center * center, axis=-1, keepdims=True) + EPS)
    return center * rstd, rstd


def norm_back(hat, rstd, gain, grad):
    scaled = grad * gain
    mean_one = jnp.mean(scaled, axis=-1, keepdims=True)
    mean_two = jnp.mean(scaled * hat, axis=-1, keepdims=True)
    return rstd * (scaled - mean_one - hat * mean_two)


def basis_of(centers, widths):
    place = lax.broadcasted_iota(jnp.int32, (DIST, 1), 0).astype(F32) * (8.0 / DIST)
    offset = (place - centers) / widths
    return offset, jnp.exp(-0.5 * offset * offset) / widths


def table_kernel(w2t_ref, w1_ref, cen_ref, wid_ref, geo_ref):
    phi = basis_of(cen_ref[...], wid_ref[...])[1].astype(BF16)
    z = dot(phi, w1_ref[...], NN)
    gz = (z * cdf(z)).astype(BF16)
    geo_ref[...] = dot(w2t_ref[...].astype(BF16), gz, NT)


def half_lanes(rows):
    return lax.broadcasted_iota(jnp.int32, (rows, 128), 1) >= 64


def splits(block, half_cols, col):
    zero = jnp.zeros_like(block)
    return jnp.concatenate(
        [jnp.where(col < half_cols, block, zero), jnp.where(col >= half_cols, block, zero)], 0
    )


def pair_masks(col, head_dim, pairs):
    head = col // head_dim
    return [jnp.logical_or(head == p, head == p + pairs) for p in range(pairs)]


def pair_stack(block, masks):
    zero = jnp.zeros_like(block)
    return jnp.concatenate([jnp.where(mask, block, zero) for mask in masks], 0)


def lookup(row, index):
    wide = jnp.broadcast_to(row, index.shape)
    return jnp.take_along_axis(wide, index, axis=1, mode="promise_in_bounds")


def forward_kernel(dims, *refs):
    mols, columns, pairs, head_dim = dims
    (where_ref, count_ref, mode_ref, x_ref, gain_ref, bias_ref, wq0, wq1, wo0, wo1) = refs[:10]
    (flat_ref, geo_ref, code_ref, part_ref, h1_ref, qkv_ref, o_ref, pt_ref) = refs[10:]
    base = where_ref[1]
    scale = 1.0 / math.sqrt(head_dim)
    hat = normed(x_ref[...].astype(F32))[0]
    h1 = (hat * gain_ref[...] + bias_ref[...]).astype(BF16)
    h1_ref[...] = h1
    for g, wq in enumerate((wq0, wq1)):
        for k in range(3):
            out = dot(h1, wq[k], NN)
            if k == 0:
                out = out * scale
            qkv_ref[3 * g + k] = out.astype(BF16)
    col = lax.broadcasted_iota(jnp.int32, (64, columns), 1)
    masks = pair_masks(col, head_dim, pairs)
    half_cols = pairs * head_dim
    half = half_lanes(64)
    row_id = lax.broadcasted_iota(jnp.int32, (64, 128), 0)

    def one(m, carry):
        rows = pl.ds(pl.multiple_of(m * 64, 64), 64)
        code = code_ref[m]
        spd_id = (code & 31) + jnp.where(half, 32, 0)
        edge_id = ((code >> 5) & 31) + jnp.where(half, 96, 64)
        dist_id = code >> 10
        keep = row_id < count_ref[base + m]
        mode = mode_ref[base + m]
        two = jnp.where(mode != 1, 1.0, 0.0).astype(F32)
        three = jnp.where(mode != 0, 1.0, 0.0).astype(F32)
        for g in range(2):
            query, keyset, values = (qkv_ref[3 * g + k, rows, :] for k in range(3))
            scores = dot(pair_stack(keyset, masks), splits(query, half_cols, col), NT)
            probs = []
            for p in range(pairs):
                flat = flat_ref[g * pairs + p : g * pairs + p + 1, :] * two
                low = geo_ref[2 * pairs * g + p : 2 * pairs * g + p + 1, :] * three
                high = geo_ref[2 * pairs * g + pairs + p : 2 * pairs * g + pairs + p + 1, :] * three
                bias = lookup(flat, spd_id) + lookup(flat, edge_id)
                bias = bias + jnp.where(half, lookup(high, dist_id), lookup(low, dist_id))
                part = jnp.where(keep, scores[p * 64 : p * 64 + 64] + bias, NEG)
                expos = jnp.exp(part - jnp.max(part, axis=0, keepdims=True))
                total = jnp.sum(expos, axis=0, keepdims=True)
                probs.append((expos / total).astype(BF16))
            probs = jnp.concatenate(probs, 0)
            pt_ref[m, g] = probs
            mixed = dot(probs, pair_stack(values, masks), TN)
            o_ref[g, rows, :] = jnp.where(col < half_cols, mixed[:64], mixed[64:]).astype(BF16)
        return carry

    lax.fori_loop(0, mols, one, 0)
    part_ref[...] = (dot(o_ref[0], wo0[...], NN) + dot(o_ref[1], wo1[...], NN)).astype(BF16)


def ffn_kernel(where_ref, *refs):
    (x_ref, pa_ref, pb_ref, c_ref, gain_ref, bias_ref, w10, w11, w20, w21) = refs[:10]
    (y1_ref, h2_ref, act_ref, ffn_ref, two_ref) = refs[10:]
    y1 = x_ref[...].astype(F32) + (pa_ref[...].astype(F32) + pb_ref[...].astype(F32))
    y1_ref[...] = y1
    h2 = (normed(y1)[0] * gain_ref[...] + bias_ref[...]).astype(BF16)
    h2_ref[...] = h2
    cot = c_ref[...]
    ffn, two = None, None
    for g, (w1, w2) in enumerate(((w10, w20), (w11, w21))):
        u = dot(h2, w1[...], NN)
        phi = cdf(u)
        act = (u * phi).astype(BF16)
        du = (dot(cot, w2[...], NT) * gelu_slope(u, phi)).astype(BF16)
        act_ref[2 * g] = act
        act_ref[2 * g + 1] = du
        one_ffn, one_two = dot(act, w2[...], NN), dot(du, w1[...], NT)
        ffn = one_ffn if ffn is None else ffn + one_ffn
        two = one_two if two is None else two + one_two
    ffn_ref[...] = ffn.astype(BF16)
    two_ref[...] = two.astype(BF16)


def ffn_grad_kernel(where_ref, *refs):
    chunks = (len(refs) - 1) // 3
    c_refs, h_refs, a_refs, out_ref = (
        refs[:chunks],
        refs[chunks : 2 * chunks],
        refs[2 * chunks : 3 * chunks],
        refs[-1],
    )
    for g in range(2):
        one, two = None, None
        for c_ref, h_ref, a_ref in zip(c_refs, h_refs, a_refs):
            more_one, more_two = dot(a_ref[2 * g + 1], h_ref[...], TN), dot(a_ref[2 * g], c_ref[...], TN)
            one = more_one if one is None else one + more_one
            two = more_two if two is None else two + more_two
        out_ref[g, 0] = one.astype(BF16)
        out_ref[g, 1] = two.astype(BF16)


def backward_kernel(dims, *refs):
    mols, columns, pairs, head_dim, share = dims
    (where_ref, mode_ref, x_ref, c_ref, y1_ref, ta_ref, tb_ref, g1_ref, g2_ref) = refs[:9]
    (wq0, wq1, wo0, wo1, code_ref, qkv_ref, pt_ref) = refs[9:16]
    (dy1_ref, gb_ref, dqkv_ref, one_ref, sums_ref, tabs_ref, do_ref, ds_ref, lhs_ref) = refs[16:]
    base = where_ref[1]
    scale = 1.0 / math.sqrt(head_dim)
    hat, rstd = normed(y1_ref[...])
    dh2 = ta_ref[...].astype(F32) + tb_ref[...].astype(F32)
    dy1 = c_ref[...].astype(F32) + norm_back(hat, rstd, g2_ref[...], dh2)
    dy1_ref[...] = dy1
    gain_two = jnp.sum(dh2 * hat, axis=0, keepdims=True) * share
    bias_two = jnp.sum(dh2, axis=0, keepdims=True) * share
    gb = dy1.astype(BF16)
    gb_ref[...] = gb
    for g, wo in enumerate((wo0, wo1)):
        do_ref[g] = dot(gb, wo[...], NT).astype(BF16)
    col = lax.broadcasted_iota(jnp.int32, (64, columns), 1)
    masks = pair_masks(col, head_dim, pairs)
    half_cols = pairs * head_dim
    heads = 4 * pairs
    low_half = jnp.logical_not(half_lanes(2 * pairs))
    low_32 = jnp.logical_not(half_lanes(32))
    row_128 = lax.broadcasted_iota(jnp.int32, (128, 128), 0)
    row_32 = lax.broadcasted_iota(jnp.int32, (32, 128), 0)
    tabs_ref[...] = jnp.zeros_like(tabs_ref)

    def own_pair(block):
        out = jnp.where(masks[0], block[:64], 0.0)
        for p in range(1, pairs):
            out = jnp.where(masks[p], block[p * 64 : p * 64 + 64], out)
        return out

    def one(m, carry):
        rows = pl.ds(pl.multiple_of(m * 64, 64), 64)
        for g in range(2):
            query, keyset, values = (qkv_ref[3 * g + k, rows, :] for k in range(3))
            grad = splits(do_ref[g, rows, :], half_cols, col)
            probs = pt_ref[m, g]
            dqkv_ref[3 * g + 2, rows, :] = own_pair(dot(probs, grad, NN)).astype(BF16)
            dprob = dot(pair_stack(values, masks), grad, NT)
            wide = probs.astype(F32)
            pieces = []
            for p in range(pairs):
                part = wide[p * 64 : p * 64 + 64]
                dp = dprob[p * 64 : p * 64 + 64]
                ds = part * (dp - jnp.sum(part * dp, axis=0, keepdims=True))
                pieces.append(ds.astype(BF16))
                ds_ref[pl.ds((g * pairs + p) * 64, 64), :] = ds
            ds = jnp.concatenate(pieces, 0)
            dq = dot(ds, pair_stack(keyset, masks), TN)
            dq = jnp.where(col < half_cols, dq[:64], dq[64:]) * scale
            dqkv_ref[3 * g, rows, :] = dq.astype(BF16)
            dk = own_pair(dot(ds, splits(query, half_cols, col), NN))
            dqkv_ref[3 * g + 1, rows, :] = dk.astype(BF16)
        code = code_ref[m]
        code = jnp.where(low_32, code[:32], code[32:])
        mode = mode_ref[base + m]
        spd_id = jnp.where(mode != 1, code & 31, -1)
        edge_id = jnp.where(mode != 1, (code >> 5) & 31, -1)
        dist_id = jnp.where(mode != 0, code >> 10, -1)
        hots = []
        for j in range(32):
            first = ds_ref[pl.ds(j, 2 * pairs, stride=64), :]
            second = ds_ref[pl.ds(j + 32, 2 * pairs, stride=64), :]
            left = jnp.where(low_half, first, pltpu.roll(second, 64, 1))
            right = jnp.where(low_half, pltpu.roll(first, 64, 1), second)
            lhs_ref[:, j * 128 : j * 128 + 128] = jnp.concatenate([left, right], 0).astype(BF16)
            hots.append(
                jnp.concatenate(
                    [
                        jnp.where(row_128 == dist_id[j : j + 1], 1.0, 0.0),
                        jnp.where(row_32 == spd_id[j : j + 1], 1.0, 0.0),
                        jnp.where(row_32 == edge_id[j : j + 1], 1.0, 0.0),
                    ],
                    0,
                ).astype(BF16)
            )
        total = None
        for j in range(0, 32, 2):
            hot = jnp.concatenate(hots[j : j + 2], 1)
            more = dot(lhs_ref[:, j * 128 : j * 128 + 256], hot, NT)
            total = more if total is None else total + more
        tabs_ref[...] += total
        return carry

    lax.fori_loop(0, mols, one, 0)
    part = None
    for g, wq in enumerate((wq0, wq1)):
        for k in range(3):
            more = dot(dqkv_ref[3 * g + k], wq[k], NT)
            part = more if part is None else part + more
    one_ref[...] = part.astype(BF16)
    hat = normed(x_ref[...].astype(F32))[0]
    sums_ref[...] = jnp.concatenate(
        [
            jnp.sum(part * hat, axis=0, keepdims=True),
            jnp.sum(part, axis=0, keepdims=True),
            gain_two,
            bias_two,
        ],
        0,
    )


def proj_grad_kernel(*refs):
    chunks = (len(refs) - 2) // 4
    h_refs, d_refs, o_refs, g_refs = (refs[i * chunks : (i + 1) * chunks] for i in range(4))
    qkv_ref, out_ref = refs[-2:]
    for g in range(2):
        for k in range(4):
            total = None
            for h_ref, d_ref, o_ref, g_ref in zip(h_refs, d_refs, o_refs, g_refs):
                if k < 3:
                    more = dot(d_ref[3 * g + k], h_ref[...], TN)
                else:
                    more = dot(o_ref[g], g_ref[...], TN)
                total = more if total is None else total + more
            if k < 3:
                qkv_ref[g, k] = total.astype(BF16)
            else:
                out_ref[g] = total.astype(BF16)


def finish_kernel(where_ref, *refs):
    x_ref, dy1_ref, a_ref, b_ref, gain_ref, out_ref = refs
    hat, rstd = normed(x_ref[...].astype(F32))
    grad = a_ref[...].astype(F32) + b_ref[...].astype(F32)
    out_ref[...] = (dy1_ref[...] + norm_back(hat, rstd, gain_ref[...], grad)).astype(BF16)


def kernel_net_kernel(geo_ref, w2_ref, w1_ref, cen_ref, wid_ref, g1_ref, g2_ref, cw_ref):
    wid = wid_ref[...]
    offset, phi = basis_of(cen_ref[...], wid)
    phi_b = phi.astype(BF16)
    z = dot(phi_b, w1_ref[...], NN)
    cum = cdf(z)
    gz = z * cum
    high = lax.Precision.HIGHEST
    dgeo = geo_ref[...]
    g2_ref[...] = lax.dot_general(dgeo, gz.astype(BF16).astype(F32), NN, precision=high)
    dgz = lax.dot_general(dgeo, w2_ref[...], TN, precision=high)
    dz = dgz * gelu_slope(z, cum)
    g1_ref[...] = lax.dot_general(phi_b.astype(F32), dz, TN, precision=high)
    dphi = lax.dot_general(dz, w1_ref[...].astype(F32), NT, precision=high)
    scaled = dphi * phi / wid
    cw_ref[...] = jnp.concatenate(
        [
            jnp.sum(scaled * offset, axis=0, keepdims=True),
            jnp.sum(scaled * (offset * offset - 1.0), axis=0, keepdims=True),
        ],
        0,
    )


def shape(dims, dtype=BF16):
    return jax.ShapeDtypeStruct(dims, dtype)


def whole(dims):
    return pl.BlockSpec(dims, lambda *_: (0,) * len(dims))


def flips(count, bit):
    return [(i, i ^ (1 << bit)) for i in range(count)]


def bits_of(count):
    return range(count.bit_length() - 1)


def body(
    hidden_in,
    w_qkv,
    w_out,
    w_ff1,
    w_ff2,
    ln1_gain,
    ln1_bias,
    ln2_gain,
    ln2_bias,
    spd_table,
    edge_table,
    kernel_w1,
    kernel_w2,
    centers,
    widths,
    atom_count,
    mol_mode,
    spd_bucket,
    edge_type,
    dist_bucket,
    cotangent,
):
    tokens, width = hidden_in.shape
    mols = spd_bucket.shape[0]
    columns = w_qkv.shape[2]
    heads = spd_table.shape[1]
    pairs = heads // 2
    head_dim = columns // heads
    tensor, data = lax.axis_size("tensor"), lax.axis_size("dp")
    t_index, d_index = lax.axis_index("tensor"), lax.axis_index("dp")
    core = t_index % 2
    my_mols = mols // 2
    n_mols = my_mols // CHUNKS
    rows = n_mols * 64

    def other(array):
        return lax.ppermute(array, "tensor", flips(tensor, 0))

    def across(array):
        for bit in list(bits_of(tensor))[1:]:
            sent = lax.ppermute(array, "tensor", flips(tensor, bit))
            if bit < tensor.bit_length() - 2:
                array = (array.astype(F32) + sent.astype(F32)).astype(BF16)
        return array, sent

    def row(vector):
        return vector.reshape(1, -1)

    gain1, bias1, gain2, bias2 = (row(v) for v in (ln1_gain, ln1_bias, ln2_gain, ln2_bias))
    cen, wid = row(centers), row(widths)
    spd_t, edge_t = spd_table.T, edge_table.T
    flat = jnp.concatenate([spd_t[:pairs], spd_t[pairs:], edge_t[:pairs], edge_t[pairs:]], 1)
    small = jnp.concatenate([flat, kernel_w2.T.astype(F32)], 0)
    small_other = other(small)
    wq_other = other(w_qkv)
    wo_other = other(w_out)
    w1_other = other(w_ff1)
    w2_other = other(w_ff2)
    w2t = jnp.concatenate([small[pairs:], small_other[pairs:]], 0)
    flat = jnp.concatenate([flat, small_other[:pairs]], 0)
    geo = pl.pallas_call(
        table_kernel, out_shape=shape((2 * heads, DIST), F32), name="bucket_table"
    )(w2t, kernel_w1, cen, wid)

    def mine(array):
        return lax.dynamic_slice_in_dim(array, core * my_mols, my_mols, 0)

    code = mine(spd_bucket) | (mine(edge_type) << 5) | (mine(dist_bucket) << 10)
    code = jnp.swapaxes(code, 1, 2)
    code = jnp.concatenate([code, code], 2)

    def place(chunk):
        return jnp.stack([core * CHUNKS + chunk, core * my_mols + chunk * n_mols]).astype(jnp.int32)

    places = [place(chunk) for chunk in range(CHUNKS)]
    row_block = pl.BlockSpec((rows, width), lambda i, at, *_: (at[0], 0))
    act_block = whole((rows, width))
    vec = whole((1, width))
    wq_spec, wo_spec = whole(w_qkv.shape), whole(w_out.shape)
    w1_spec, w2_spec = whole(w_ff1.shape), whole(w_ff2.shape)
    qkv_spec, o_spec = whole((6, rows, columns)), whole((2, rows, columns))
    pt_spec = whole((n_mols, 2, pairs * 64, 128))

    def code_spec(chunk):
        return pl.BlockSpec((n_mols, 64, 128), lambda i, *_: (chunk, 0, 0))

    def call(kernel, scalars, ins, outs, shapes, name, scratch=()):
        spec = pltpu.PrefetchScalarGridSpec(
            num_scalar_prefetch=len(scalars), grid=(1,), in_specs=ins, out_specs=outs, scratch_shapes=list(scratch)
        )
        return pl.pallas_call(kernel, grid_spec=spec, out_shape=shapes, name=name)

    dims = (n_mols, columns, pairs, head_dim)
    parts, h1s, qkvs, os_, pts, crossed = [], [], [], [], [], []
    for chunk in range(CHUNKS):
        scalars = (places[chunk], atom_count, mol_mode)
        part, h1, qkv, mixed, probs = call(
            lambda *refs: forward_kernel(dims, *refs),
            scalars,
            [row_block, vec, vec, wq_spec, wq_spec, wo_spec, wo_spec]
            + [whole(flat.shape), whole(geo.shape), code_spec(chunk)],
            [act_block, act_block, qkv_spec, o_spec, pt_spec],
            [
                shape((rows, width)),
                shape((rows, width)),
                shape((6, rows, columns)),
                shape((2, rows, columns)),
                shape((n_mols, 2, pairs * 64, 128)),
            ],
            "attend",
        )(*scalars, hidden_in, gain1, bias1, w_qkv, wq_other, w_out, wo_other, flat, geo, code)
        h1s.append(h1), qkvs.append(qkv), os_.append(mixed), pts.append(probs)
        crossed.append(across(part))

    y1s, h2s, acts, ffns, twos = [], [], [], [], []
    for chunk in range(CHUNKS):
        y1, h2, act, ffn, two = call(
            ffn_kernel,
            (places[chunk],),
            [row_block, act_block, act_block, row_block, vec, vec, w1_spec, w1_spec, w2_spec, w2_spec],
            [act_block, act_block, whole((4, rows, columns)), act_block, act_block],
            [
                shape((rows, width), F32),
                shape((rows, width)),
                shape((4, rows, columns)),
                shape((rows, width)),
                shape((rows, width)),
            ],
            "ffn",
        )(places[chunk], hidden_in, *crossed[chunk], cotangent, gain2, bias2, w_ff1, w1_other, w_ff2, w2_other)
        y1s.append(y1), h2s.append(h2), acts.append(act), ffns.append(ffn)
        twos.append(across(two))

    c_block = pl.BlockSpec((rows, width), lambda i, at, *_: (at[0], 0))
    c_specs = [
        pl.BlockSpec((rows, width), lambda i, at, chunk=chunk: (at[0] + chunk, 0)) for chunk in range(CHUNKS)
    ]
    ff_grads = call(
        ffn_grad_kernel,
        (places[0],),
        c_specs + [act_block] * CHUNKS + [whole((4, rows, columns))] * CHUNKS,
        [whole((2, 2, columns, width))],
        [shape((2, 2, columns, width))],
        "ffn_grad",
    )(places[0], *([cotangent] * CHUNKS), *h2s, *acts)[0]

    dims = (n_mols, columns, pairs, head_dim, 2.0 / tensor)
    dy1s, gbs, dqkvs, ones, sums, tabs = [], [], [], [], None, None
    for chunk in range(CHUNKS):
        dy1, gb, dqkv, one, some, tab = call(
            lambda *refs: backward_kernel(dims, *refs),
            (places[chunk], mol_mode),
            [row_block, row_block, act_block, act_block, act_block, vec, vec]
            + [wq_spec, wq_spec, wo_spec, wo_spec, code_spec(chunk), qkv_spec, pt_spec],
            [act_block, act_block, qkv_spec, act_block, whole((4, width)), whole((2 * heads, 192))],
            [
                shape((rows, width), F32),
                shape((rows, width)),
                shape((6, rows, columns)),
                shape((rows, width)),
                shape((4, width), F32),
                shape((2 * heads, 192), F32),
            ],
            "attend_back",
            [
                pltpu.VMEM((2, rows, columns), BF16),
                pltpu.VMEM((2 * pairs * 64, 128), F32),
                pltpu.VMEM((2 * heads, 32 * 128), BF16),
            ],
        )(
            places[chunk], mol_mode, hidden_in, cotangent, y1s[chunk], *twos[chunk], gain1, gain2,
            w_qkv, wq_other, w_out, wo_other, code, qkvs[chunk], pts[chunk],
        )
        dy1s.append(dy1), gbs.append(gb), dqkvs.append(dqkv)
        ones.append(across(one))
        sums = some if sums is None else sums + some
        tabs = tab if tabs is None else tabs + tab

    qkv_grads, out_grads = pl.pallas_call(
        proj_grad_kernel,
        out_shape=[shape((2, 3, columns, width)), shape((2, columns, width))],
        name="proj_grad",
    )(*h1s, *dqkvs, *os_, *gbs)

    def reduced(grads):
        grads = grads.reshape(2, -1, width)
        got = other(grads[1])
        array = (grads[0].astype(F32) + got.astype(F32)).astype(BF16)
        for bit in bits_of(data):
            size = array.shape[0] // 2
            side = (d_index >> bit) & 1
            sent = lax.dynamic_slice_in_dim(array, (1 - side) * size, size, 0)
            kept = lax.dynamic_slice_in_dim(array, side * size, size, 0)
            got = lax.ppermute(sent, "dp", flips(data, bit))
            array = (kept.astype(F32) + got.astype(F32)).astype(BF16)
        for bit in reversed(bits_of(data)):
            got = lax.ppermute(array, "dp", flips(data, bit))
            side = (d_index >> bit) & 1
            array = jnp.where(
                side == 0, jnp.concatenate([array, got], 0), jnp.concatenate([got, array], 0)
            )
        return array.reshape(-1, columns, width).astype(F32)

    ff_sum = reduced(ff_grads)
    out_sum = reduced(out_grads)
    qkv_sum = reduced(qkv_grads)

    table = jnp.zeros((heads * tensor, 192), F32)
    table = lax.dynamic_update_slice_in_dim(table, heads_of(tabs, 0, heads, pairs), t_index * heads, 0)
    table = lax.dynamic_update_slice_in_dim(table, heads_of(tabs, 1, heads, pairs), (t_index ^ 1) * heads, 0)
    w2_full = jnp.zeros((heads * tensor, 128), F32)
    w2_full = lax.dynamic_update_slice_in_dim(w2_full, small[pairs:], t_index * heads, 0)
    for bit in bits_of(tensor):
        w2_full = w2_full + lax.ppermute(w2_full, "tensor", flips(tensor, bit))
    packed = jnp.concatenate([table, sums.reshape(-1, 192)], 0)
    for bit in bits_of(tensor):
        packed = packed + lax.ppermute(packed, "tensor", flips(tensor, bit))
    for bit in bits_of(data):
        packed = packed + lax.ppermute(packed, "dp", flips(data, bit))
    table, sums = packed[: heads * tensor], packed[heads * tensor :].reshape(4, width)
    grad_kw1, grad_kw2, grad_cw = pl.pallas_call(
        kernel_net_kernel,
        out_shape=[shape((128, 128), F32), shape((heads * tensor, 128), F32), shape((2, 128), F32)],
        name="kernel_net",
    )(table[:, :DIST], w2_full, kernel_w1, cen, wid)
    own = lax.dynamic_slice_in_dim(table, t_index * heads, heads, 0).T
    grad_kw2 = lax.dynamic_slice_in_dim(grad_kw2, t_index * heads, heads, 0).T

    finals, outs = [], []
    for chunk in range(CHUNKS):
        finals.append(
            call(
                finish_kernel,
                (places[chunk],),
                [row_block, act_block, act_block, act_block, vec],
                act_block,
                shape((rows, width)),
                "finish",
            )(places[chunk], hidden_in, dy1s[chunk], *ones[chunk], gain1)
        )
        ffn_a, ffn_b = across(ffns[chunk])
        outs.append((y1s[chunk] + (ffn_a.astype(F32) + ffn_b.astype(F32))).astype(BF16))

    def joined(pieces):
        piece = jnp.concatenate(pieces, 0)
        got = other(piece)
        return jnp.where(core == 0, jnp.concatenate([piece, got], 0), jnp.concatenate([got, piece], 0))

    return (
        joined(outs),
        joined(finals),
        jnp.swapaxes(qkv_sum, 1, 2),
        out_sum[0],
        ff_sum[0].T,
        ff_sum[1],
        sums[0],
        sums[1],
        sums[2],
        sums[3],
        own[DIST : DIST + SPD],
        own[DIST + SPD :],
        grad_kw1,
        grad_kw2,
        grad_cw[0],
        grad_cw[1],
    )


def heads_of(tabs, group, heads, pairs):
    view = tabs.reshape(2, 2, pairs, tabs.shape[1])
    return view[:, group].reshape(heads, tabs.shape[1])


def solution(mesh):
    in_specs = (
        P("dp", None),
        P(None, None, "tensor"),
        P("tensor", None),
        P(None, "tensor"),
        P("tensor", None),
        P(),
        P(),
        P(),
        P(),
        P(None, "tensor"),
        P(None, "tensor"),
        P(),
        P(None, "tensor"),
        P(),
        P(),
        P("dp"),
        P("dp"),
        P("dp", None, None),
        P("dp", None, None),
        P("dp", None, None),
        P("dp", None),
    )
    out_specs = (
        P("dp", None),
        P("dp", None),
        P(None, None, "tensor"),
        P("tensor", None),
        P(None, "tensor"),
        P("tensor", None),
        P(),
        P(),
        P(),
        P(),
        P(None, "tensor"),
        P(None, "tensor"),
        P(),
        P(None, "tensor"),
        P(),
        P(),
    )
    return jax.shard_map(body, mesh=mesh, in_specs=in_specs, out_specs=out_specs, check_vma=False)
```
